256 devices in a mesh: leaf: 256 (over z, y, x, core).
Axes of the slice: x: 4, y: 4, z: 8, core: 2. Of those that a mesh axis runs over, the one named last changes fastest.
Arguments:
- samples: float32 [131072, 1024], P('leaf'), may hold values from -6 to 6
- test_vectors: float32 [131072, 1024], P('leaf'), may hold values from -6 to 6
- diag_blocks: float32 [131072, 512], P('leaf'), may hold values from -0.25 to 0.25
- leaf_skeleton: int32 [256, 128], P('leaf'), may hold values from 0 to 511, as said below
- leaf_rank: int32 [256], replicated, may hold values from 64 to 128, as said below
- coupling_1: float32 [32768, 128], P('leaf'), may hold values from -0.5 to 0.5
- coupling_2: float32 [16384, 128], P('leaf'), may hold values from -0.5 to 0.5
- coupling_3: float32 [8192, 128], P('leaf'), may hold values from -0.5 to 0.5
- skeleton_1: int32 [128, 128], replicated, may hold values from 0 to 255, as said below
- rank_1: int32 [128], replicated, may hold values from 64 to 128, as said below
- skeleton_2: int32 [64, 128], replicated, may hold values from 0 to 255, as said below
- rank_2: int32 [64], replicated, may hold values from 64 to 128, as said below
- skeleton_3: int32 [32, 128], replicated, may hold values from 0 to 255, as said below
- rank_3: int32 [32], replicated, may hold values from 64 to 128, as said below
Outputs:
- leaf_basis: float32 [131072, 128], P('leaf')
- basis_1: float32 [32768, 128], P('leaf')
- basis_2: float32 [16384, 128], P('leaf')
- basis_3: float32 [8192, 128], P('leaf')
- top_samples: float32 [4096, 1024], P('leaf')
- top_projected: float32 [4096, 1024], P('leaf')
The draws below stay inside these ranges and needn't reach their ends.
Inputs may be any that keep to these rules, and one draw needn't show every extreme that they name: `leaf_skeleton`: each row lists 128 different ports of its leaf. Only the first leaf_rank[n] entries of skeleton row n count; some leaf has rank 128 and some 128 // 2. `skeleton_1`: row n lists 128 different rows of node n's stacked samples (rows below 128 from the first child, the rest from the second); its first rank_1[n] entries are live rows, below the child's rank within its half. `rank_1`: some node has rank 128 and some 128 // 2. `skeleton_2`: as skeleton_1, for level 2 nodes. `rank_2`: some node has rank 128 and some 128 // 2. `skeleton_3`: as skeleton_1, for level 3 nodes. `rank_3`: some node has rank 128 and some 128 // 2.
All inputs are finite; a program needn't handle non-finite values.
Results may differ from the reference program's by a relative error of at most 0.0003.
Values sent between devices are 32-bit elements; how exact they have to be, the bound alone decides.
A program may use at most 64 MiB of HBM per device.

```python
import jax
import jax.numpy as jnp
from jax import lax

LEAF = 512
SAMPLES = 1024
KMAX = 128
LEAVES = 256


def level_ranks(key):
    node_counts = (LEAVES, LEAVES // 2, LEAVES // 4, LEAVES // 8)
    tables = []
    for level_id in range(4):
        level_key = jax.random.fold_in(jax.random.fold_in(key, 7), level_id)
        node_count = node_counts[level_id]
        values = jax.random.randint(jax.random.fold_in(level_key, 0), (node_count,), KMAX // 2, KMAX + 1)
        top_at = jax.random.randint(jax.random.fold_in(level_key, 1), (), 0, node_count)
        low_at = (top_at + 1 + jax.random.randint(jax.random.fold_in(level_key, 2), (), 0, node_count - 1)) % node_count
        values = values.at[top_at].set(KMAX).at[low_at].set(KMAX // 2)
        tables.append(values.astype(jnp.int32))
    return tables


def level_skeleton(key, level_id):
    child_ranks = level_ranks(key)[level_id - 1].reshape(2, -1).T
    node_keys = jax.random.split(jax.random.fold_in(key, 100 + level_id), child_ranks.shape[0])
    position = jnp.arange(2 * KMAX)

    def one_node(node_key, pair_rank):
        shuffled = jax.random.permutation(node_key, 2 * KMAX)
        dead_rows = jnp.where(position < KMAX, position >= pair_rank[0], position - KMAX >= pair_rank[1])
        scores = shuffled + 2 * KMAX * dead_rows.astype(jnp.int32)
        return jnp.argsort(scores)[:KMAX]
    return jax.vmap(one_node)(node_keys, child_ranks).astype(jnp.int32)


def draw_leaf_skeleton(key, part):
    leaf_keys = jax.random.split(jax.random.fold_in(key, 50), LEAVES)
    return jax.vmap(lambda leaf_key: jax.random.permutation(leaf_key, LEAF)[:KMAX])(leaf_keys).astype(jnp.int32)


def draw_leaf_rank(key, part):
    return level_ranks(key)[0]


def draw_rank_1(key, part):
    return level_ranks(key)[1]


def draw_rank_2(key, part):
    return level_ranks(key)[2]


def draw_rank_3(key, part):
    return level_ranks(key)[3]


def draw_skeleton_1(key, part):
    return level_skeleton(key, 1)


def draw_skeleton_2(key, part):
    return level_skeleton(key, 2)


def draw_skeleton_3(key, part):
    return level_skeleton(key, 3)


def level_of(own_key, shape, pieces, least, largest):
    level, own = 1.0, jax.random.fold_in(own_key, 6)
    for axis_at, blocks in pieces:
        heights = jnp.exp(jax.random.uniform(jax.random.fold_in(own, axis_at), (blocks,), jnp.float32, least / len(pieces), largest / len(pieces)))
        level = level * jnp.repeat(heights, shape[axis_at] // blocks).reshape([-1 if axis == axis_at else 1 for axis in range(len(shape))])
    return level


def centred(key, dims, scale, most, pieces=(), kind=jnp.bfloat16):
    result = scale * jax.random.normal(key, dims, jnp.float32)
    if pieces:
        result = result * level_of(key, dims, pieces, -0.22, 0.18)
    return jnp.clip(result, -most, most).astype(kind)


def setup_inputs(seed: int = 0) -> dict:
    keys = jax.random.split(jax.random.key(seed), 15)
    return {
        "samples": centred(keys[0], (LEAVES * LEAF, SAMPLES), 1.0, 6.0, ((0, 256),), jnp.float32),
        "test_vectors": centred(keys[1], (LEAVES * LEAF, SAMPLES), 1.0, 6.0, ((0, 256),), jnp.float32),
        "diag_blocks": centred(keys[2], (LEAVES * LEAF, LEAF), LEAF ** -0.5, 0.25, ((0, 256),), jnp.float32),
        "leaf_skeleton": draw_leaf_skeleton(jax.random.fold_in(keys[14], 71), 0),
        "leaf_rank": draw_leaf_rank(jax.random.fold_in(keys[14], 71), 0),
        "coupling_1": centred(keys[5], (LEAVES * KMAX, KMAX), KMAX ** -0.5, 0.5, ((0, 256),), jnp.float32),
        "coupling_2": centred(keys[6], (LEAVES * KMAX // 2, KMAX), KMAX ** -0.5, 0.5, ((0, 256),), jnp.float32),
        "coupling_3": centred(keys[7], (LEAVES * KMAX // 4, KMAX), KMAX ** -0.5, 0.5, ((0, 256),), jnp.float32),
        "skeleton_1": draw_skeleton_1(jax.random.fold_in(keys[14], 71), 0),
        "rank_1": draw_rank_1(jax.random.fold_in(keys[14], 71), 0),
        "skeleton_2": draw_skeleton_2(jax.random.fold_in(keys[14], 71), 0),
        "rank_2": draw_rank_2(jax.random.fold_in(keys[14], 71), 0),
        "skeleton_3": draw_skeleton_3(jax.random.fold_in(keys[14], 71), 0),
        "rank_3": draw_rank_3(jax.random.fold_in(keys[14], 71), 0),
    }


HIGH = lax.Precision.HIGHEST

def select_rows(matrix, skeleton, rank_now):
    live_rows = (jnp.arange(skeleton.shape[0]) < rank_now).astype(jnp.float32)
    return jnp.take(matrix, skeleton.astype(jnp.int32), axis=0) * live_rows[:, None]

def factorize(chosen, rank_now):
    gram_matrix = jnp.dot(chosen, chosen.T, precision=HIGH)
    ridge_term = 0.5 * jnp.sum(chosen * chosen) / rank_now.astype(jnp.float32) + 1e-06
    system = gram_matrix + ridge_term * jnp.eye(chosen.shape[0], dtype=jnp.float32)
    return jnp.linalg.cholesky(system)

def solve_rows(row_block, chosen, factor):
    cross_terms = jnp.dot(row_block, chosen.T, precision=HIGH)
    return jax.scipy.linalg.cho_solve((factor, True), cross_terms.T).T

def merge_level(chosen, projected, child_rank, coupling, skeleton, rank_level, level_id):
    pairs = chosen.shape[0] // 2
    group_size = 2 ** level_id
    block_rows = 2 * KMAX // group_size
    chosen_pairs = chosen.reshape(2, pairs, KMAX, SAMPLES).transpose(1, 0, 2, 3)
    proj_pairs = projected.reshape(2, pairs, KMAX, SAMPLES).transpose(1, 0, 2, 3)
    rank_pairs = child_rank.reshape(2, pairs).T
    blocks = coupling.reshape(group_size // 2, 2, pairs, block_rows, KMAX).transpose(2, 1, 0, 3, 4).reshape(pairs, 2, KMAX, KMAX)

    def node_work(items):
        chosen_two, proj_two, rank_two, block_two, skeleton_row, rank_now = items
        row_index = jnp.arange(KMAX)
        first_rows = chosen_two[0] - jnp.dot(block_two[0], proj_two[1], precision=HIGH)
        second_rows = chosen_two[1] - jnp.dot(block_two[1], proj_two[0], precision=HIGH)
        first_rows = first_rows * (row_index < rank_two[0]).astype(jnp.float32)[:, None]
        second_rows = second_rows * (row_index < rank_two[1]).astype(jnp.float32)[:, None]
        stacked = jnp.concatenate([first_rows, second_rows], axis=0)
        chosen_new = select_rows(stacked, skeleton_row, rank_now)
        factor = factorize(chosen_new, rank_now)
        basis_rows = solve_rows(stacked, chosen_new, factor)
        both_proj = jnp.concatenate([proj_two[0], proj_two[1]], axis=0)
        proj_new = jnp.dot(basis_rows.T, both_proj, precision=HIGH)
        return (chosen_new, basis_rows, proj_new)
    chosen_new, basis_nodes, proj_new = lax.map(node_work, (chosen_pairs, proj_pairs, rank_pairs, blocks, skeleton, rank_level))
    basis_out = basis_nodes.reshape(pairs, 2, group_size // 2, block_rows, KMAX).transpose(2, 1, 0, 3, 4).reshape(-1, KMAX)
    return (chosen_new, basis_out, proj_new)

def top_layout(values):
    nodes = values.shape[0]
    return values.reshape(nodes, 8, KMAX // 8, SAMPLES).transpose(1, 0, 2, 3).reshape(-1, SAMPLES)

def reference(samples, test_vectors, diag_blocks, leaf_skeleton, leaf_rank, coupling_1, coupling_2, coupling_3, skeleton_1, rank_1, skeleton_2, rank_2, skeleton_3, rank_3):

    def leaf_work(items):
        rows_sampled, omega_rows, diag_block, skeleton_row, rank_now = items
        local_rows = rows_sampled - jnp.dot(diag_block, omega_rows, precision=HIGH)
        chosen = select_rows(local_rows, skeleton_row, rank_now)
        factor = factorize(chosen, rank_now)
        basis_rows = solve_rows(local_rows, chosen, factor)
        return (chosen, basis_rows, jnp.dot(basis_rows.T, omega_rows, precision=HIGH))
    chosen, leaf_basis, projected = lax.map(leaf_work, (samples.reshape(LEAVES, LEAF, SAMPLES), test_vectors.reshape(LEAVES, LEAF, SAMPLES), diag_blocks.reshape(LEAVES, LEAF, LEAF), leaf_skeleton, leaf_rank))
    chosen, basis_one, projected = merge_level(chosen, projected, leaf_rank, coupling_1, skeleton_1, rank_1, 1)
    chosen, basis_two, projected = merge_level(chosen, projected, rank_1, coupling_2, skeleton_2, rank_2, 2)
    chosen, basis_three, projected = merge_level(chosen, projected, rank_2, coupling_3, skeleton_3, rank_3, 3)
    return (leaf_basis.reshape(LEAVES * LEAF, KMAX), basis_one, basis_two, basis_three, top_layout(chosen), top_layout(projected))
```

```python
import jax
import jax.numpy as jnp
from jax import lax
from jax.experimental import pallas as pl
from jax.experimental.pallas import tpu as pltpu
from jax.sharding import PartitionSpec as P

RING = 8
K = 128
LEAF = 512
SAMPLES = 1024
CHUNK = 256
STEPS = SAMPLES // CHUNK
F32 = jnp.float32
BF16 = jnp.bfloat16
NN = (((1,), (0,)), ((), ()))
NT = (((1,), (1,)), ((), ()))


def dot(left, right, dims=NN):
    return lax.dot_general(left, right, dims, preferred_element_type=F32)


def split(value):
    high = value.astype(BF16)
    low = (value - high.astype(F32)).astype(BF16)
    return high, low


def dot3(left, right, dims=NN):
    small = dot(left[0], right[1], dims) + dot(left[1], right[0], dims)
    return dot(left[0], right[0], dims) + small


def spread_ratios(count):
    ratios = [2.0 * K + 1.0]
    for _ in range(count):
        last = ratios[-1]
        ratios.append((last + 1.0) ** 2 / (4.0 * last))
    return ratios


def inverse(gram, rank):
    row = lax.broadcasted_iota(jnp.int32, (K, K), 0)
    col = lax.broadcasted_iota(jnp.int32, (K, K), 1)
    eye = jnp.where(row == col, 1.0, 0.0).astype(F32)
    total = jnp.sum(jnp.sum(gram * eye, axis=0, keepdims=True), axis=1, keepdims=True)
    ridge = 0.5 * total / rank + 1e-06
    shrink = 1.0 / ridge
    system = gram * shrink + eye
    ratios = spread_ratios(6)
    parts = split(system)
    first = ratios[0]
    approx = ((first + 1.0) * eye - system) * (1.0 / first)
    product = ((first + 1.0) * system - dot3(parts, parts)) * (1.0 / first)
    for step in range(1, 6):
        ratio = ratios[step]
        factor = split(((ratio + 1.0) * eye - product) * (1.0 / ratio))
        approx = dot3(split(approx), factor)
        if step < 5:
            product = dot3(split(product), factor)
    approx = approx * (2.0 / (1.0 + ratios[6]))
    residual = eye - lax.dot_general(
        system, approx, NN, precision=lax.Precision.HIGHEST, preferred_element_type=F32
    )
    approx = approx + dot3(split(approx), split(residual))
    return approx * shrink


def selector(skeleton_row, rank, width):
    wide = jnp.transpose(jnp.broadcast_to(skeleton_row, (K, K)))
    live = lax.broadcasted_iota(jnp.int32, (K, K), 0) < rank
    blocks = []
    for block in range(width // K):
        want = lax.broadcasted_iota(jnp.int32, (K, K), 1) + block * K
        blocks.append(jnp.where((wide == want) & live, 1.0, 0.0).astype(BF16))
    return jnp.concatenate(blocks, axis=1)


def body(
    stride,
    samples,
    tests,
    diag,
    leaf_skeleton,
    skeleton_1,
    skeleton_2,
    skeleton_3,
    coupling_1,
    coupling_2,
    coupling_3,
    leaf_rank,
    rank_1,
    rank_2,
    rank_3,
    leaf_basis,
    basis_1,
    basis_2,
    basis_3,
    top_samples,
    top_projected,
    s_buf,
    w_buf,
    d_buf,
    d_high,
    d_low,
    w_high,
    w_low,
    out_c,
    out_p,
    c_1,
    p_1,
    c_2,
    p_2,
    c_3,
    p_3,
    c_top,
    p_top,
    e_1,
    e_2,
    e_3,
    kept_high,
    kept_low,
    basis_leaf,
    basis_buf_1,
    basis_buf_2,
    basis_buf_3,
    load_sem,
    leaf_out_sem,
    e_send,
    e_recv_1,
    e_recv_2,
    e_recv_3,
    c_send,
    p_send,
    c_recv_1,
    p_recv_1,
    c_recv_2,
    p_recv_2,
    c_recv_3,
    p_recv_3,
    out_send_1,
    out_send_2,
    out_send_3,
    top_send_c,
    top_send_p,
    out_recv,
):
    device = lax.axis_index("leaf")
    rest = device % stride
    z = device // stride
    shift = (rest % 2) * (RING // 2)
    pos = (z + RING - shift) % RING

    def at_z(where):
        return where * stride + rest

    def at_pos(where):
        return at_z((where + shift) % RING)

    def remote(src, dst, send, recv, target):
        return pltpu.make_async_remote_copy(
            src_ref=src,
            dst_ref=dst,
            send_sem=send,
            recv_sem=recv,
            device_id=(target,),
            device_id_type=pl.DeviceIdType.MESH,
        )

    def push(src, dst, send, recv, target):
        @pl.when(target != device)
        def _():
            remote(src, dst, send, recv, target).start()

        @pl.when(target == device)
        def _():
            pltpu.make_async_copy(src, dst, recv).start()

    def pushed(src, dst, send, recv, target):
        @pl.when(target != device)
        def _():
            remote(src, dst, send, recv, target).wait_send()

    def arrived(dst, recv):
        pltpu.make_async_copy(dst, dst, recv).wait()

    load_d = pltpu.make_async_copy(diag, d_buf, load_sem.at[0])
    load_d.start()
    loads_w, loads_s = [], []
    for k in range(STEPS):
        span = pl.ds(k * CHUNK, CHUNK)
        loads_w.append(pltpu.make_async_copy(tests.at[:, span], w_buf.at[k], load_sem.at[1 + 2 * k]))
        loads_s.append(pltpu.make_async_copy(samples.at[:, span], s_buf.at[k], load_sem.at[2 + 2 * k]))
        loads_w[k].start()
        loads_s[k].start()

    barrier = pltpu.get_barrier_semaphore()
    for hop in range(1, RING):
        pl.semaphore_signal(
            barrier,
            inc=1,
            device_id=(at_z((z + hop) % RING),),
            device_id_type=pl.DeviceIdType.MESH,
        )

    node_leaf = z % 4
    child_leaf = z // 4
    home_1 = at_pos(node_leaf // 2 + 2 * (1 - node_leaf % 2))
    node_1 = 2 * (pos % 2) + 1 - (pos % 4) // 2
    node_2 = node_1 % 2
    child_1 = pos % 2
    home_2 = at_pos(2 - node_2)
    child_2 = node_2
    home_3 = at_pos(1)

    select = selector(leaf_skeleton[...], leaf_rank[device], LEAF)
    load_d.wait()
    for r in range(4):
        rows = pl.ds(r * K, K)
        high, low = split(d_buf[rows, :])
        d_high[rows, :] = high
        d_low[rows, :] = low

    home_e2 = at_pos(2 - z % 2)
    c2, h2 = (z // 2) % 2, z // 4
    c3, h3 = z % 2, z // 2
    moves_e = (
        (coupling_1, e_1.at[child_leaf], e_send.at[0], e_recv_1.at[child_leaf], home_1),
        (
            coupling_2,
            e_2.at[c2, pl.ds(pl.multiple_of(h2 * 64, 64), 64)],
            e_send.at[1],
            e_recv_2.at[c2, h2],
            home_e2,
        ),
        (
            coupling_3,
            e_3.at[c3, pl.ds(pl.multiple_of(h3 * 32, 32), 32)],
            e_send.at[2],
            e_recv_3.at[c3, h3],
            home_3,
        ),
    )

    cross = [jnp.zeros((K, K), F32) for _ in range(4)]
    gram = jnp.zeros((K, K), F32)
    moves_c, moves_p = [], []
    for k in range(STEPS):
        loads_w[k].wait()
        loads_s[k].wait()
        high, low = split(w_buf[k])
        w_high[k] = high
        w_low[k] = low
        w_parts = (w_high[k], w_low[k])
        parts = []
        chosen_high = jnp.zeros((K, CHUNK), F32)
        chosen_low = jnp.zeros((K, CHUNK), F32)
        for r in range(4):
            rows = pl.ds(r * K, K)
            local = s_buf[k, rows, :] - dot3((d_high[rows, :], d_low[rows, :]), w_parts)
            part = split(local)
            parts.append(part)
            columns = select[:, r * K : (r + 1) * K]
            chosen_high = chosen_high + dot(columns, part[0])
            chosen_low = chosen_low + dot(columns, part[1])
        out_c[k] = chosen_high + chosen_low
        if k == 0:
            pl.semaphore_wait(barrier, RING - 1)
            for move in moves_e:
                push(*move)
        moves_c.append(
            remote(
                out_c.at[k],
                c_1.at[child_leaf, k],
                c_send.at[0, k],
                c_recv_1.at[child_leaf, k],
                home_1,
            )
        )
        moves_c[k].start()
        chosen = (chosen_high.astype(BF16), chosen_low.astype(BF16))
        for r in range(4):
            cross[r] = cross[r] + dot3(chosen, parts[r], NT)
        gram = gram + dot3(chosen, chosen, NT)

    inv = split(inverse(gram, leaf_rank[device].astype(F32)))
    basis_rows = [dot3(inv, split(cross[r])) for r in range(4)]
    basis_parts = [split(rows) for rows in basis_rows]
    for k in range(STEPS):
        total = jnp.zeros((K, CHUNK), F32)
        for r in range(4):
            rows = pl.ds(r * K, K)
            total = total + dot3(basis_parts[r], (w_high[k, rows, :], w_low[k, rows, :]))
        out_p[k] = total
        moves_p.append(
            remote(
                out_p.at[k],
                p_1.at[child_leaf, k],
                p_send.at[0, k],
                p_recv_1.at[child_leaf, k],
                home_1,
            )
        )
        moves_p[k].start()
    for r in range(4):
        basis_leaf[pl.ds(r * K, K), :] = jnp.transpose(basis_rows[r])
    leaf_out = pltpu.make_async_copy(basis_leaf, leaf_basis, leaf_out_sem)
    leaf_out.start()

    def merge(c_in, p_in, e_in, wait_e, wait_c, wait_p, skeleton_row, rank, rank_a, rank_b, emit_c, emit_p):
        choose = selector(skeleton_row, rank, 2 * K)
        row = lax.broadcasted_iota(jnp.int32, (K, CHUNK), 0)
        mask_a = (row < rank_a).astype(F32)
        mask_b = (row < rank_b).astype(F32)
        wait_e()
        e_top = split(e_in[0])
        e_bottom = split(e_in[1])
        cross_node = jnp.zeros((K, 2 * K), F32)
        gram_node = jnp.zeros((K, K), F32)
        for k in range(STEPS):
            wait_c(k)
            wait_p(k)
            first = split(p_in[0, k])
            second = split(p_in[1, k])
            for child, part in ((0, first), (1, second)):
                kept_high[k, pl.ds(child * K, K), :] = part[0]
                kept_low[k, pl.ds(child * K, K), :] = part[1]
            top = (c_in[0, k] - dot3(e_top, second)) * mask_a
            bottom = (c_in[1, k] - dot3(e_bottom, first)) * mask_b
            stacked = split(jnp.concatenate([top, bottom], axis=0))
            chosen_high = dot(choose, stacked[0])
            chosen_low = dot(choose, stacked[1])
            emit_c(k, chosen_high + chosen_low)
            chosen = (chosen_high.astype(BF16), chosen_low.astype(BF16))
            cross_node = cross_node + dot3(chosen, stacked, NT)
            gram_node = gram_node + dot3(chosen, chosen, NT)
        inv_node = split(inverse(gram_node, rank.astype(F32)))
        basis_node = dot3(inv_node, split(cross_node))
        node_parts = split(basis_node)
        for k in range(STEPS):
            emit_p(k, dot3(node_parts, (kept_high[k], kept_low[k])))
        return jnp.concatenate(
            [jnp.transpose(basis_node[:, :K]), jnp.transpose(basis_node[:, K:])], axis=0
        )

    @pl.when(pos < 4)
    def _():
        id_1 = at_z(node_1)

        def wait_e():
            for child in range(2):
                arrived(e_1.at[child], e_recv_1.at[child])

        def wait_c(k):
            for child in range(2):
                arrived(c_1.at[child, k], c_recv_1.at[child, k])

        def wait_p(k):
            for child in range(2):
                arrived(p_1.at[child, k], p_recv_1.at[child, k])

        def send(buf, sends, recvs, k):
            return remote(buf.at[child_1, k], buf.at[child_1, k], sends.at[1, k], recvs.at[k], home_2)

        def emit_c(k, value):
            c_2[child_1, k] = value

            @pl.when(home_2 != device)
            def _():
                send(c_2, c_send, c_recv_2, k).start()

        def emit_p(k, value):
            p_2[child_1, k] = value

            @pl.when(home_2 != device)
            def _():
                send(p_2, p_send, p_recv_2, k).start()

        basis_buf_1[...] = merge(
            c_1,
            p_1,
            e_1,
            wait_e,
            wait_c,
            wait_p,
            skeleton_1[pl.ds(id_1, 1), :],
            rank_1[id_1],
            leaf_rank[id_1],
            leaf_rank[at_z(node_1 + 4)],
            emit_c,
            emit_p,
        )
        for c in range(2):
            remote(
                basis_buf_1.at[pl.ds(c * K, K)],
                basis_1,
                out_send_1.at[c],
                out_recv.at[0],
                at_z(node_1 + 4 * c),
            ).start()

    is_2 = (pos == 1) | (pos == 2)

    @pl.when(is_2)
    def _():
        id_2 = at_z(node_2)
        other = 1 - child_1

        def wait_e():
            for c in range(2):
                for h in range(2):
                    arrived(e_2.at[c, pl.ds(h * 64, 64)], e_recv_2.at[c, h])

        def wait_c(k):
            arrived(c_2.at[other, k], c_recv_2.at[k])

        def wait_p(k):
            arrived(p_2.at[other, k], p_recv_2.at[k])

        def send(buf, sends, recvs, k):
            return remote(buf.at[child_2, k], buf.at[child_2, k], sends.at[2, k], recvs.at[k], home_3)

        def emit_c(k, value):
            c_3[child_2, k] = value

            @pl.when(home_3 != device)
            def _():
                send(c_3, c_send, c_recv_3, k).start()

        def emit_p(k, value):
            p_3[child_2, k] = value

            @pl.when(home_3 != device)
            def _():
                send(p_3, p_send, p_recv_3, k).start()

        basis_buf_2[...] = merge(
            c_2,
            p_2,
            e_2,
            wait_e,
            wait_c,
            wait_p,
            skeleton_2[pl.ds(id_2, 1), :],
            rank_2[id_2],
            rank_1[id_2],
            rank_1[at_z(node_2 + 2)],
            emit_c,
            emit_p,
        )
        for c in range(2):
            for h in range(2):
                push(
                    basis_buf_2.at[pl.ds(c * K + h * 64, 64)],
                    basis_2,
                    out_send_2.at[c, h],
                    out_recv.at[1],
                    at_z(node_2 + 2 * (2 * h + c)),
                )

    @pl.when(pos == 1)
    def _():
        def wait_e():
            for c in range(2):
                for h in range(4):
                    arrived(e_3.at[c, pl.ds(h * 32, 32)], e_recv_3.at[c, h])

        def wait_c(k):
            arrived(c_3.at[0, k], c_recv_3.at[k])

        def wait_p(k):
            arrived(p_3.at[0, k], p_recv_3.at[k])

        def emit_c(k, value):
            c_top[:, pl.ds(k * CHUNK, CHUNK)] = value
            if k == STEPS - 1:
                for j in range(RING):
                    push(
                        c_top.at[pl.ds(j * 16, 16)],
                        top_samples,
                        top_send_c.at[j],
                        out_recv.at[3],
                        at_z(j),
                    )

        def emit_p(k, value):
            p_top[:, pl.ds(k * CHUNK, CHUNK)] = value
            if k == STEPS - 1:
                for j in range(RING):
                    push(
                        p_top.at[pl.ds(j * 16, 16)],
                        top_projected,
                        top_send_p.at[j],
                        out_recv.at[4],
                        at_z(j),
                    )

        basis_buf_3[...] = merge(
            c_3,
            p_3,
            e_3,
            wait_e,
            wait_c,
            wait_p,
            skeleton_3[pl.ds(rest, 1), :],
            rank_3[rest],
            rank_2[rest],
            rank_2[at_z(1)],
            emit_c,
            emit_p,
        )
        for c in range(2):
            for h in range(4):
                push(
                    basis_buf_3.at[pl.ds(c * K + h * 32, 32)],
                    basis_3,
                    out_send_3.at[c, h],
                    out_recv.at[2],
                    at_z(2 * h + c),
                )

    for move in moves_c + moves_p:
        move.wait_send()
    for move in moves_e:
        pushed(*move)
    leaf_out.wait()

    @pl.when(pos < 4)
    def _():
        @pl.when(home_2 != device)
        def _():
            for k in range(STEPS):
                for buf, sends, recvs in ((c_2, c_send, c_recv_2), (p_2, p_send, p_recv_2)):
                    remote(
                        buf.at[child_1, k], buf.at[child_1, k], sends.at[1, k], recvs.at[k], home_2
                    ).wait_send()

        for c in range(2):
            remote(
                basis_buf_1.at[pl.ds(c * K, K)],
                basis_1,
                out_send_1.at[c],
                out_recv.at[0],
                at_z(node_1 + 4 * c),
            ).wait_send()

    @pl.when(is_2)
    def _():
        @pl.when(home_3 != device)
        def _():
            for k in range(STEPS):
                for buf, sends, recvs in ((c_3, c_send, c_recv_3), (p_3, p_send, p_recv_3)):
                    remote(
                        buf.at[child_2, k], buf.at[child_2, k], sends.at[2, k], recvs.at[k], home_3
                    ).wait_send()

        for c in range(2):
            for h in range(2):
                pushed(
                    basis_buf_2.at[pl.ds(c * K + h * 64, 64)],
                    basis_2,
                    out_send_2.at[c, h],
                    out_recv.at[1],
                    at_z(node_2 + 2 * (2 * h + c)),
                )

    @pl.when(pos == 1)
    def _():
        for j in range(RING):
            pushed(
                c_top.at[pl.ds(j * 16, 16)], top_samples, top_send_c.at[j], out_recv.at[3], at_z(j)
            )
            pushed(
                p_top.at[pl.ds(j * 16, 16)], top_projected, top_send_p.at[j], out_recv.at[4], at_z(j)
            )
        for c in range(2):
            for h in range(4):
                pushed(
                    basis_buf_3.at[pl.ds(c * K + h * 32, 32)],
                    basis_3,
                    out_send_3.at[c, h],
                    out_recv.at[2],
                    at_z(2 * h + c),
                )

    arrived(basis_1, out_recv.at[0])
    arrived(basis_2, out_recv.at[1])
    arrived(basis_3, out_recv.at[2])
    arrived(top_samples, out_recv.at[3])
    arrived(top_projected, out_recv.at[4])


def shards(
    samples,
    test_vectors,
    diag_blocks,
    leaf_skeleton,
    leaf_rank,
    coupling_1,
    coupling_2,
    coupling_3,
    skeleton_1,
    rank_1,
    skeleton_2,
    rank_2,
    skeleton_3,
    rank_3,
):
    stride = lax.axis_size("leaf") // RING
    hbm = pl.BlockSpec(memory_space=pltpu.MemorySpace.HBM)
    vmem = pl.BlockSpec(memory_space=pltpu.MemorySpace.VMEM)
    smem = pl.BlockSpec(memory_space=pltpu.MemorySpace.SMEM)
    dma = pltpu.SemaphoreType.DMA
    slots = pltpu.VMEM((2, STEPS, K, CHUNK), F32)
    blocks = pltpu.VMEM((STEPS, K, CHUNK), F32)

    def kernel(*refs):
        body(stride, *refs)

    return pl.pallas_call(
        kernel,
        name="hss_tree",
        out_shape=(
            jax.ShapeDtypeStruct((LEAF, K), F32),
            jax.ShapeDtypeStruct((K, K), F32),
            jax.ShapeDtypeStruct((K // 2, K), F32),
            jax.ShapeDtypeStruct((K // 4, K), F32),
            jax.ShapeDtypeStruct((K // 8, SAMPLES), F32),
            jax.ShapeDtypeStruct((K // 8, SAMPLES), F32),
        ),
        in_specs=[hbm] * 3 + [vmem] * 7 + [smem] * 4,
        out_specs=(hbm,) * 6,
        scratch_shapes=[
            pltpu.VMEM((STEPS, LEAF, CHUNK), F32),
            pltpu.VMEM((STEPS, LEAF, CHUNK), F32),
            pltpu.VMEM((LEAF, LEAF), F32),
            pltpu.VMEM((LEAF, LEAF), BF16),
            pltpu.VMEM((LEAF, LEAF), BF16),
            pltpu.VMEM((STEPS, LEAF, CHUNK), BF16),
            pltpu.VMEM((STEPS, LEAF, CHUNK), BF16),
            blocks,
            blocks,
            slots,
            slots,
            slots,
            slots,
            slots,
            slots,
            pltpu.VMEM((K, SAMPLES), F32),
            pltpu.VMEM((K, SAMPLES), F32),
            pltpu.VMEM((2, K, K), F32),
            pltpu.VMEM((2, K, K), F32),
            pltpu.VMEM((2, K, K), F32),
            pltpu.VMEM((STEPS, 2 * K, CHUNK), BF16),
            pltpu.VMEM((STEPS, 2 * K, CHUNK), BF16),
            pltpu.VMEM((LEAF, K), F32),
            pltpu.VMEM((2 * K, K), F32),
            pltpu.VMEM((2 * K, K), F32),
            pltpu.VMEM((2 * K, K), F32),
            dma((1 + 2 * STEPS,)),
            dma(()),
            dma((3,)),
            dma((2,)),
            dma((2, 2)),
            dma((2, 4)),
            dma((3, STEPS)),
            dma((3, STEPS)),
            dma((2, STEPS)),
            dma((2, STEPS)),
            dma((STEPS,)),
            dma((STEPS,)),
            dma((STEPS,)),
            dma((STEPS,)),
            dma((2,)),
            dma((2, 2)),
            dma((2, 4)),
            dma((RING,)),
            dma((RING,)),
            dma((5,)),
        ],
        compiler_params=pltpu.CompilerParams(
            collective_id=0, has_side_effects=True, vmem_limit_bytes=48 * 1024 * 1024
        ),
    )(
        samples,
        test_vectors,
        diag_blocks,
        leaf_skeleton,
        skeleton_1,
        skeleton_2,
        skeleton_3,
        coupling_1,
        coupling_2,
        coupling_3,
        leaf_rank,
        rank_1,
        rank_2,
        rank_3,
    )


def solution(mesh):
    rows = P("leaf", None)
    return jax.shard_map(
        shards,
        mesh=mesh,
        in_specs=(rows,) * 4 + (P(),) + (rows,) * 3 + (P(),) * 6,
        out_specs=(rows,) * 6,
        check_vma=False,
    )
```

```python
import jax
import jax.numpy as jnp
from jax import lax
from jax.experimental import pallas as pl
from jax.experimental.pallas import tpu as pltpu
from jax.sharding import PartitionSpec as P

RING = 8
K = 128
LEAF = 512
SAMPLES = 1024
CHUNK = 256
STEPS = SAMPLES // CHUNK
F32 = jnp.float32
BF16 = jnp.bfloat16
NN = (((1,), (0,)), ((), ()))
NT = (((1,), (1,)), ((), ()))


def dot(left, right, dims=NN):
    return lax.dot_general(left, right, dims, preferred_element_type=F32)


def split(value):
    high = value.astype(BF16)
    low = (value - high.astype(F32)).astype(BF16)
    return high, low


def dot3(left, right, dims=NN):
    small = dot(left[0], right[1], dims) + dot(left[1], right[0], dims)
    return dot(left[0], right[0], dims) + small


def spread_ratios(count):
    ratios = [2.0 * K + 1.0]
    for _ in range(count):
        last = ratios[-1]
        ratios.append((last + 1.0) ** 2 / (4.0 * last))
    return ratios


def inverse(gram, rank):
    row = lax.broadcasted_iota(jnp.int32, (K, K), 0)
    col = lax.broadcasted_iota(jnp.int32, (K, K), 1)
    eye = jnp.where(row == col, 1.0, 0.0).astype(F32)
    total = jnp.sum(jnp.sum(gram * eye, axis=0, keepdims=True), axis=1, keepdims=True)
    ridge = 0.5 * total / rank + 1e-06
    shrink = 1.0 / ridge
    system = gram * shrink + eye
    ratios = spread_ratios(6)
    parts = split(system)
    first = ratios[0]
    approx = ((first + 1.0) * eye - system) * (1.0 / first)
    product = ((first + 1.0) * system - dot3(parts, parts)) * (1.0 / first)
    for step in range(1, 6):
        ratio = ratios[step]
        factor = split(((ratio + 1.0) * eye - product) * (1.0 / ratio))
        approx = dot3(split(approx), factor)
        if step < 5:
            product = dot3(split(product), factor)
    approx = approx * (2.0 / (1.0 + ratios[6]))
    residual = eye - lax.dot_general(
        system, approx, NN, precision=lax.Precision.HIGHEST, preferred_element_type=F32
    )
    approx = approx + dot3(split(approx), split(residual))
    return approx * shrink


def selector(skeleton_row, rank, width):
    wide = jnp.transpose(jnp.broadcast_to(skeleton_row, (K, K)))
    live = lax.broadcasted_iota(jnp.int32, (K, K), 0) < rank
    blocks = []
    for block in range(width // K):
        want = lax.broadcasted_iota(jnp.int32, (K, K), 1) + block * K
        blocks.append(jnp.where((wide == want) & live, 1.0, 0.0).astype(BF16))
    return jnp.concatenate(blocks, axis=1)


def products(stack, rows, chosen_high, chosen_low):
    stack[2 * rows : 2 * rows + K, :] = chosen_high.astype(BF16)
    stack[2 * rows + K :, :] = chosen_low.astype(BF16)
    both = dot(stack[...], stack[2 * rows :, :], NT)
    cross = both[:rows, :K] + (both[:rows, K:] + both[rows : 2 * rows, :K])
    low_left = both[2 * rows + K :, :K]
    gram = both[2 * rows : 2 * rows + K, :K] + (both[2 * rows : 2 * rows + K, K:] + low_left)
    return cross, gram


def times(left, right):
    rows = left[0].shape[0]
    both = dot(jnp.concatenate(left, axis=0), jnp.concatenate(split(right), axis=1))
    return both[:rows, :K] + (both[:rows, K:] + both[rows:, :K])


def finish(*refs):
    count = len(refs) // 3
    sources, results, spare = refs[:count], refs[count : 2 * count], refs[2 * count : 3 * count]
    sems = refs[3 * count]
    loads = [
        pltpu.make_async_copy(sources[i], spare[i], sems.at[0, i]) for i in range(count)
    ]
    stores = [
        pltpu.make_async_copy(spare[i], results[i], sems.at[1, i]) for i in range(count)
    ]
    for load in loads:
        load.start()
    for load, store in zip(loads, stores):
        load.wait()
        store.start()
    for store in stores:
        store.wait()


def body(
    stride,
    samples,
    tests,
    diag,
    leaf_skeleton,
    skeleton_1,
    skeleton_2,
    skeleton_3,
    coupling_1,
    coupling_2,
    coupling_3,
    leaf_rank,
    rank_1,
    rank_2,
    rank_3,
    leaf_basis,
    basis_1,
    basis_2,
    basis_3,
    top_samples,
    top_projected,
    s_buf,
    w_buf,
    d_buf,
    d_parts,
    w_high,
    w_low,
    out_c,
    out_p,
    c_1,
    p_1,
    c_2,
    p_2,
    c_3,
    p_3,
    c_top,
    p_top,
    e_1,
    e_2,
    e_3,
    kept_high,
    kept_low,
    stack_leaf,
    stack_node,
    cross_leaf,
    basis_leaf,
    basis_buf_1,
    basis_buf_2,
    basis_buf_3,
    load_sem,
    leaf_out_sem,
    e_send,
    e_recv_1,
    e_recv_2,
    e_recv_3,
    c_send,
    p_send,
    c_recv_1,
    p_recv_1,
    c_recv_2,
    p_recv_2,
    c_recv_3,
    p_recv_3,
    out_send_1,
    out_send_2,
    out_send_3,
    top_send_c,
    top_send_p,
    out_recv,
):
    device = lax.axis_index("leaf")
    rest = device % stride
    z = device // stride
    shift = (rest % 2) * (RING // 2)
    pos = (z + RING - shift) % RING

    def at_z(where):
        return where * stride + rest

    def at_pos(where):
        return at_z((where + shift) % RING)

    def remote(src, dst, send, recv, target):
        return pltpu.make_async_remote_copy(
            src_ref=src,
            dst_ref=dst,
            send_sem=send,
            recv_sem=recv,
            device_id=(target,),
            device_id_type=pl.DeviceIdType.MESH,
        )

    def push(src, dst, send, recv, target):
        @pl.when(target != device)
        def _():
            remote(src, dst, send, recv, target).start()

        @pl.when(target == device)
        def _():
            pltpu.make_async_copy(src, dst, recv).start()

    def pushed(src, dst, send, recv, target):
        @pl.when(target != device)
        def _():
            remote(src, dst, send, recv, target).wait_send()

    def arrived(dst, recv):
        pltpu.make_async_copy(dst, dst, recv).wait()

    load_d = pltpu.make_async_copy(diag, d_buf, load_sem.at[0])
    load_d.start()
    loads_w, loads_s = [], []
    for k in range(STEPS):
        span = pl.ds(k * CHUNK, CHUNK)
        loads_w.append(pltpu.make_async_copy(tests.at[:, span], w_buf.at[k], load_sem.at[1 + 2 * k]))
        loads_s.append(pltpu.make_async_copy(samples.at[:, span], s_buf.at[k], load_sem.at[2 + 2 * k]))
        loads_w[k].start()
        loads_s[k].start()

    barrier = pltpu.get_barrier_semaphore()
    for hop in range(1, RING):
        pl.semaphore_signal(
            barrier,
            inc=1,
            device_id=(at_z((z + hop) % RING),),
            device_id_type=pl.DeviceIdType.MESH,
        )

    node_leaf = z % 4
    child_leaf = z // 4
    home_1 = at_pos(node_leaf // 2 + 2 * (1 - node_leaf % 2))
    node_1 = 2 * (pos % 2) + 1 - (pos % 4) // 2
    node_2 = node_1 % 2
    child_1 = pos % 2
    home_2 = at_pos(2 - node_2)
    child_2 = node_2
    home_3 = at_pos(1)

    select = selector(leaf_skeleton[...], leaf_rank[device], LEAF)
    load_d.wait()
    high, low = split(d_buf[...])
    d_parts[:LEAF, :] = high
    d_parts[LEAF:, :] = low

    home_e2 = at_pos(2 - z % 2)
    c2, h2 = (z // 2) % 2, z // 4
    c3, h3 = z % 2, z // 2
    moves_e = (
        (coupling_1, e_1.at[child_leaf], e_send.at[0], e_recv_1.at[child_leaf], home_1),
        (
            coupling_2,
            e_2.at[c2, pl.ds(pl.multiple_of(h2 * 64, 64), 64)],
            e_send.at[1],
            e_recv_2.at[c2, h2],
            home_e2,
        ),
        (
            coupling_3,
            e_3.at[c3, pl.ds(pl.multiple_of(h3 * 32, 32), 32)],
            e_send.at[2],
            e_recv_3.at[c3, h3],
            home_3,
        ),
    )

    gram = jnp.zeros((K, K), F32)
    moves_c, moves_p = [], []
    for k in range(STEPS):
        loads_w[k].wait()
        loads_s[k].wait()
        high, low = split(w_buf[k])
        w_high[k] = high
        w_low[k] = low
        both = dot(d_parts[...], w_high[k])
        local = s_buf[k] - (both[:LEAF] + (both[LEAF:] + dot(d_parts[:LEAF, :], w_low[k])))
        high, low = split(local)
        stack_leaf[:LEAF, :] = high
        stack_leaf[LEAF : 2 * LEAF, :] = low
        chosen_high = dot(select, stack_leaf[:LEAF, :])
        chosen_low = dot(select, stack_leaf[LEAF : 2 * LEAF, :])
        out_c[k] = chosen_high + chosen_low
        if k == 0:
            pl.semaphore_wait(barrier, RING - 1)
            for move in moves_e:
                push(*move)
        moves_c.append(
            remote(
                out_c.at[k],
                c_1.at[child_leaf, k],
                c_send.at[0, k],
                c_recv_1.at[child_leaf, k],
                home_1,
            )
        )
        moves_c[k].start()
        term, gram_term = products(stack_leaf, LEAF, chosen_high, chosen_low)
        gram = gram + gram_term
        if k == 0:
            cross_leaf[...] = term
        else:
            cross_leaf[...] += term

    basis = times(split(cross_leaf[...]), inverse(gram, leaf_rank[device].astype(F32)))
    turned = jnp.concatenate(split(jnp.transpose(basis)), axis=0)
    for k in range(STEPS):
        both = dot(turned, w_high[k])
        out_p[k] = both[:K] + (both[K:] + dot(turned[:K], w_low[k]))
        moves_p.append(
            remote(
                out_p.at[k],
                p_1.at[child_leaf, k],
                p_send.at[0, k],
                p_recv_1.at[child_leaf, k],
                home_1,
            )
        )
        moves_p[k].start()
    basis_leaf[...] = basis
    leaf_out = pltpu.make_async_copy(basis_leaf, leaf_basis, leaf_out_sem)
    leaf_out.start()

    def merge(c_in, p_in, e_in, wait_e, wait_c, wait_p, skeleton_row, rank, rank_a, rank_b, emit_c, emit_p):
        choose = selector(skeleton_row, rank, 2 * K)
        row = lax.broadcasted_iota(jnp.int32, (2 * K, CHUNK), 0)
        live = row < jnp.where(row < K, rank_a, K + rank_b)
        wait_e()
        zero = jnp.zeros((K, K), BF16)
        top = split(e_in[0])
        bottom = split(e_in[1])
        cross_parts = [
            jnp.concatenate(
                [
                    jnp.concatenate([zero, top[part]], axis=1),
                    jnp.concatenate([bottom[part], zero], axis=1),
                ],
                axis=0,
            )
            for part in range(2)
        ]
        couple = jnp.concatenate(cross_parts, axis=0)
        cross = jnp.zeros((2 * K, K), F32)
        gram_node = jnp.zeros((K, K), F32)
        for k in range(STEPS):
            wait_c(k)
            wait_p(k)
            for child in range(2):
                part = split(p_in[child, k])
                kept_high[k, pl.ds(child * K, K), :] = part[0]
                kept_low[k, pl.ds(child * K, K), :] = part[1]
            both = dot(couple, kept_high[k])
            change = both[: 2 * K] + (both[2 * K :] + dot(cross_parts[0], kept_low[k]))
            stacked = jnp.concatenate([c_in[0, k], c_in[1, k]], axis=0) - change
            high, low = split(jnp.where(live, stacked, 0.0))
            stack_node[: 2 * K, :] = high
            stack_node[2 * K : 4 * K, :] = low
            chosen_high = dot(choose, high)
            chosen_low = dot(choose, low)
            emit_c(k, chosen_high + chosen_low)
            term, gram_term = products(stack_node, 2 * K, chosen_high, chosen_low)
            cross = cross + term
            gram_node = gram_node + gram_term
        basis = times(split(cross), inverse(gram_node, rank.astype(F32)))
        turned = jnp.concatenate(split(jnp.transpose(basis)), axis=0)
        for k in range(STEPS):
            both = dot(turned, kept_high[k])
            emit_p(k, both[:K] + (both[K:] + dot(turned[:K], kept_low[k])))
        return basis

    @pl.when(pos < 4)
    def _():
        id_1 = at_z(node_1)

        def wait_e():
            for child in range(2):
                arrived(e_1.at[child], e_recv_1.at[child])

        def wait_c(k):
            for child in range(2):
                arrived(c_1.at[child, k], c_recv_1.at[child, k])

        def wait_p(k):
            for child in range(2):
                arrived(p_1.at[child, k], p_recv_1.at[child, k])

        def send(buf, sends, recvs, k):
            return remote(buf.at[child_1, k], buf.at[child_1, k], sends.at[1, k], recvs.at[k], home_2)

        def emit_c(k, value):
            c_2[child_1, k] = value

            @pl.when(home_2 != device)
            def _():
                send(c_2, c_send, c_recv_2, k).start()

        def emit_p(k, value):
            p_2[child_1, k] = value

            @pl.when(home_2 != device)
            def _():
                send(p_2, p_send, p_recv_2, k).start()

        basis_buf_1[...] = merge(
            c_1,
            p_1,
            e_1,
            wait_e,
            wait_c,
            wait_p,
            skeleton_1[pl.ds(id_1, 1), :],
            rank_1[id_1],
            leaf_rank[id_1],
            leaf_rank[at_z(node_1 + 4)],
            emit_c,
            emit_p,
        )
        for c in range(2):
            remote(
                basis_buf_1.at[pl.ds(c * K, K)],
                basis_1,
                out_send_1.at[c],
                out_recv.at[0],
                at_z(node_1 + 4 * c),
            ).start()

    is_2 = (pos == 1) | (pos == 2)

    @pl.when(is_2)
    def _():
        id_2 = at_z(node_2)
        other = 1 - child_1

        def wait_e():
            for c in range(2):
                for h in range(2):
                    arrived(e_2.at[c, pl.ds(h * 64, 64)], e_recv_2.at[c, h])

        def wait_c(k):
            arrived(c_2.at[other, k], c_recv_2.at[k])

        def wait_p(k):
            arrived(p_2.at[other, k], p_recv_2.at[k])

        def send(buf, sends, recvs, k):
            return remote(buf.at[child_2, k], buf.at[child_2, k], sends.at[2, k], recvs.at[k], home_3)

        def emit_c(k, value):
            c_3[child_2, k] = value

            @pl.when(home_3 != device)
            def _():
                send(c_3, c_send, c_recv_3, k).start()

        def emit_p(k, value):
            p_3[child_2, k] = value

            @pl.when(home_3 != device)
            def _():
                send(p_3, p_send, p_recv_3, k).start()

        basis_buf_2[...] = merge(
            c_2,
            p_2,
            e_2,
            wait_e,
            wait_c,
            wait_p,
            skeleton_2[pl.ds(id_2, 1), :],
            rank_2[id_2],
            rank_1[id_2],
            rank_1[at_z(node_2 + 2)],
            emit_c,
            emit_p,
        )
        for c in range(2):
            for h in range(2):
                push(
                    basis_buf_2.at[pl.ds(c * K + h * 64, 64)],
                    basis_2,
                    out_send_2.at[c, h],
                    out_recv.at[1],
                    at_z(node_2 + 2 * (2 * h + c)),
                )

    @pl.when(pos == 1)
    def _():
        def wait_e():
            for c in range(2):
                for h in range(4):
                    arrived(e_3.at[c, pl.ds(h * 32, 32)], e_recv_3.at[c, h])

        def wait_c(k):
            arrived(c_3.at[0, k], c_recv_3.at[k])

        def wait_p(k):
            arrived(p_3.at[0, k], p_recv_3.at[k])

        def emit_c(k, value):
            c_top[:, pl.ds(k * CHUNK, CHUNK)] = value
            if k == STEPS - 1:
                for j in range(RING):
                    push(
                        c_top.at[pl.ds(j * 16, 16)],
                        top_samples,
                        top_send_c.at[j],
                        out_recv.at[3],
                        at_z(j),
                    )

        def emit_p(k, value):
            p_top[:, pl.ds(k * CHUNK, CHUNK)] = value
            if k == STEPS - 1:
                for j in range(RING):
                    push(
                        p_top.at[pl.ds(j * 16, 16)],
                        top_projected,
                        top_send_p.at[j],
                        out_recv.at[4],
                        at_z(j),
                    )

        basis_buf_3[...] = merge(
            c_3,
            p_3,
            e_3,
            wait_e,
            wait_c,
            wait_p,
            skeleton_3[pl.ds(rest, 1), :],
            rank_3[rest],
            rank_2[rest],
            rank_2[at_z(1)],
            emit_c,
            emit_p,
        )
        for c in range(2):
            for h in range(4):
                push(
                    basis_buf_3.at[pl.ds(c * K + h * 32, 32)],
                    basis_3,
                    out_send_3.at[c, h],
                    out_recv.at[2],
                    at_z(2 * h + c),
                )

    for move in moves_c + moves_p:
        move.wait_send()
    for move in moves_e:
        pushed(*move)
    leaf_out.wait()

    @pl.when(pos < 4)
    def _():
        @pl.when(home_2 != device)
        def _():
            for k in range(STEPS):
                for buf, sends, recvs in ((c_2, c_send, c_recv_2), (p_2, p_send, p_recv_2)):
                    remote(
                        buf.at[child_1, k], buf.at[child_1, k], sends.at[1, k], recvs.at[k], home_2
                    ).wait_send()

        for c in range(2):
            remote(
                basis_buf_1.at[pl.ds(c * K, K)],
                basis_1,
                out_send_1.at[c],
                out_recv.at[0],
                at_z(node_1 + 4 * c),
            ).wait_send()

    @pl.when(is_2)
    def _():
        @pl.when(home_3 != device)
        def _():
            for k in range(STEPS):
                for buf, sends, recvs in ((c_3, c_send, c_recv_3), (p_3, p_send, p_recv_3)):
                    remote(
                        buf.at[child_2, k], buf.at[child_2, k], sends.at[2, k], recvs.at[k], home_3
                    ).wait_send()

        for c in range(2):
            for h in range(2):
                pushed(
                    basis_buf_2.at[pl.ds(c * K + h * 64, 64)],
                    basis_2,
                    out_send_2.at[c, h],
                    out_recv.at[1],
                    at_z(node_2 + 2 * (2 * h + c)),
                )

    @pl.when(pos == 1)
    def _():
        for j in range(RING):
            pushed(
                c_top.at[pl.ds(j * 16, 16)], top_samples, top_send_c.at[j], out_recv.at[3], at_z(j)
            )
            pushed(
                p_top.at[pl.ds(j * 16, 16)], top_projected, top_send_p.at[j], out_recv.at[4], at_z(j)
            )
        for c in range(2):
            for h in range(4):
                pushed(
                    basis_buf_3.at[pl.ds(c * K + h * 32, 32)],
                    basis_3,
                    out_send_3.at[c, h],
                    out_recv.at[2],
                    at_z(2 * h + c),
                )

    arrived(basis_1, out_recv.at[0])
    arrived(basis_2, out_recv.at[1])
    arrived(basis_3, out_recv.at[2])
    arrived(top_samples, out_recv.at[3])
    arrived(top_projected, out_recv.at[4])


def shards(
    samples,
    test_vectors,
    diag_blocks,
    leaf_skeleton,
    leaf_rank,
    coupling_1,
    coupling_2,
    coupling_3,
    skeleton_1,
    rank_1,
    skeleton_2,
    rank_2,
    skeleton_3,
    rank_3,
):
    stride = lax.axis_size("leaf") // RING
    hbm = pl.BlockSpec(memory_space=pltpu.MemorySpace.HBM)
    vmem = pl.BlockSpec(memory_space=pltpu.MemorySpace.VMEM)
    smem = pl.BlockSpec(memory_space=pltpu.MemorySpace.SMEM)
    dma = pltpu.SemaphoreType.DMA
    slots = pltpu.VMEM((2, STEPS, K, CHUNK), F32)
    blocks = pltpu.VMEM((STEPS, K, CHUNK), F32)

    def kernel(*refs):
        body(stride, *refs)

    shapes = ((LEAF, K), (K, K), (K // 2, K), (K // 4, K), (K // 8, SAMPLES), (K // 8, SAMPLES))
    results = tuple(jax.ShapeDtypeStruct(shape, F32) for shape in shapes)
    values = pl.pallas_call(
        kernel,
        name="hss_tree",
        out_shape=results,
        in_specs=[hbm] * 3 + [vmem] * 7 + [smem] * 4,
        out_specs=(hbm,) * 6,
        scratch_shapes=[
            pltpu.VMEM((STEPS, LEAF, CHUNK), F32),
            pltpu.VMEM((STEPS, LEAF, CHUNK), F32),
            pltpu.VMEM((LEAF, LEAF), F32),
            pltpu.VMEM((2 * LEAF, LEAF), BF16),
            pltpu.VMEM((STEPS, LEAF, CHUNK), BF16),
            pltpu.VMEM((STEPS, LEAF, CHUNK), BF16),
            blocks,
            blocks,
            slots,
            slots,
            slots,
            slots,
            slots,
            slots,
            pltpu.VMEM((K, SAMPLES), F32),
            pltpu.VMEM((K, SAMPLES), F32),
            pltpu.VMEM((2, K, K), F32),
            pltpu.VMEM((2, K, K), F32),
            pltpu.VMEM((2, K, K), F32),
            pltpu.VMEM((STEPS, 2 * K, CHUNK), BF16),
            pltpu.VMEM((STEPS, 2 * K, CHUNK), BF16),
            pltpu.VMEM((2 * LEAF + 2 * K, CHUNK), BF16),
            pltpu.VMEM((6 * K, CHUNK), BF16),
            pltpu.VMEM((LEAF, K), F32),
            pltpu.VMEM((LEAF, K), F32),
            pltpu.VMEM((2 * K, K), F32),
            pltpu.VMEM((2 * K, K), F32),
            pltpu.VMEM((2 * K, K), F32),
            dma((1 + 2 * STEPS,)),
            dma(()),
            dma((3,)),
            dma((2,)),
            dma((2, 2)),
            dma((2, 4)),
            dma((3, STEPS)),
            dma((3, STEPS)),
            dma((2, STEPS)),
            dma((2, STEPS)),
            dma((STEPS,)),
            dma((STEPS,)),
            dma((STEPS,)),
            dma((STEPS,)),
            dma((2,)),
            dma((2, 2)),
            dma((2, 4)),
            dma((RING,)),
            dma((RING,)),
            dma((5,)),
        ],
        compiler_params=pltpu.CompilerParams(
            collective_id=0, has_side_effects=True, vmem_limit_bytes=67043328
        ),
    )(
        samples,
        test_vectors,
        diag_blocks,
        leaf_skeleton,
        skeleton_1,
        skeleton_2,
        skeleton_3,
        coupling_1,
        coupling_2,
        coupling_3,
        leaf_rank,
        rank_1,
        rank_2,
        rank_3,
    )
    return pl.pallas_call(
        finish,
        name="hss_finish",
        out_shape=results,
        in_specs=[hbm] * 6,
        out_specs=(hbm,) * 6,
        scratch_shapes=[pltpu.VMEM(shape, F32) for shape in shapes] + [dma((2, 6))],
        compiler_params=pltpu.CompilerParams(vmem_limit_bytes=67043328),
    )(*values)


def solution(mesh):
    rows = P("leaf", None)
    return jax.shard_map(
        shards,
        mesh=mesh,
        in_specs=(rows,) * 4 + (P(),) + (rows,) * 3 + (P(),) * 6,
        out_specs=(rows,) * 6,
        check_vma=False,
    )
```
